256 devices in a mesh: dp: 64 (over x, z, core), mp: 4 (over y).
Axes of the slice: x: 4, y: 4, z: 8, core: 2. Of those that a mesh axis runs over, the one named last changes fastest.
Arguments:
- inputs: bfloat16 [49152, 4608], P('dp'), may hold values from -8 to 8
- key_cotangent: bfloat16 [49152, 2048], P('dp', 'mp'), may hold values from -8 to 8
- master: float32 [4608, 2048], P('dp', 'mp'), may hold values from -0.09375 to 0.09375
- first_codes: int32 [4608, 2048], P('dp', 'mp'), may hold values from -127 to 127
- second_codes: int32 [4608, 2048], P('dp', 'mp'), may hold values from 1 to 255
- first_scale: float32 [1152, 4], P('dp', 'mp'), may hold values from 0.05 to 0.5
- second_scale: float32 [1152, 4], P('dp', 'mp'), may hold values from 0.02 to 0.2
Outputs:
- weight: bfloat16 [4608, 2048], P(None, 'mp')
- new_master: float32 [4608, 2048], P('dp', 'mp')
- first_unit: float32 [4608, 2048], P('dp', 'mp')
- second_unit: float32 [4608, 2048], P('dp', 'mp')
- first_top: float32 [1152, 4], P('dp', 'mp')
- second_top: float32 [1152, 4], P('dp', 'mp')
The draws below stay inside these ranges and needn't reach their ends.
All inputs are finite; a program needn't handle non-finite values. Where the reference program divides by a largest or mean magnitude, that divisor is 1e-20 or more.
Results may differ from the reference program's by a relative error of at most 0.0004.
Values may be sent and summed in bfloat16 or wider, within the bound.
No kernel may reach another device: no remote copies, remote signals or barrier semaphores. Data moves between devices by JAX's collectives and lax.ppermute only.
A program may use at most 128 MiB of HBM per device.

```python
import math
import jax
import jax.numpy as jnp
from jax import lax

D = 4608
KV = 2048
QROWS = 4
QCOLS = 512
STEP = 10
TOKENS = 49152
N_DP = 64
N_MP = 4


def column_levels(key, width_total, groups):
    key_order, key_texture = jax.random.split(key, 2)
    ordering = jax.random.permutation(key_order, groups)
    ladder = jnp.exp(jnp.linspace(-0.6, 0.6, groups, dtype=jnp.float32))
    levels = ladder[ordering]
    texture = jax.random.uniform(key_texture, (width_total,), jnp.float32, minval=0.6, maxval=1.4)
    return jnp.repeat(levels, width_total // groups) * texture


def shaped_field(key, row_total, width_total, groups):
    key_level, key_main = jax.random.split(jax.random.fold_in(key, 17), 2)
    scales = column_levels(key_level, width_total, groups)
    normal_part = jax.random.normal(key_main, (row_total, width_total), jnp.float32)
    values = normal_part * scales[None, :]
    return jnp.clip(values, -8.0, 8.0).astype(jnp.bfloat16)


def draw_inputs(key, part):
    return shaped_field(jax.random.fold_in(key, 1), TOKENS, D, N_DP)


def draw_key_cotangent(key, part):
    return shaped_field(jax.random.fold_in(key, 2), TOKENS, KV, N_MP)


def set_ends(entries, own_key, smallest, high):
    index_at = [jax.random.randint(jax.random.fold_in(own_key, axis), (), 0, length) for axis, length in enumerate(entries.shape)]
    main_axis = entries.shape.index(max(entries.shape))
    beside = index_at[:main_axis] + [(index_at[main_axis] + 1) % entries.shape[main_axis]] + index_at[main_axis + 1:]
    return entries.at[tuple(index_at)].set(smallest).at[tuple(beside)].set(high)


def level_of(key, extent, shards, least, largest):
    gain, own = 1.0, jax.random.fold_in(key, 6)
    for dim, shards_of in shards:
        draws = jnp.exp(jax.random.uniform(jax.random.fold_in(own, dim), (shards_of,), jnp.float32, least / len(shards), largest / len(shards)))
        gain = gain * jnp.repeat(draws, extent[dim] // shards_of).reshape([-1 if axis == dim else 1 for axis in range(len(extent))])
    return gain


def centred(key, shape, width, reach, cuts=(), kind=jnp.bfloat16):
    drawn = width * jax.random.normal(key, shape, jnp.float32)
    if cuts:
        drawn = drawn * level_of(key, shape, cuts, -0.22, 0.18)
    return jnp.clip(drawn, -reach, reach).astype(kind)


def setup_inputs(seed: int = 0) -> dict:
    splits = jax.random.split(jax.random.key(seed), 8)
    return {
        "inputs": draw_inputs(jax.random.fold_in(splits[7], 71), 0),
        "key_cotangent": draw_key_cotangent(jax.random.fold_in(splits[7], 71), 0),
        "master": centred(splits[2], (D, KV), D ** -0.5, 0.09375, ((0, 64), (1, 4)), jnp.float32),
        "first_codes": set_ends(jax.random.randint(splits[3], (D, KV), -127, 128), jax.random.fold_in(splits[3], 1), -127, 127).astype(jnp.int32),
        "second_codes": set_ends(jax.random.randint(splits[4], (D, KV), 1, 256), jax.random.fold_in(splits[4], 1), 1, 255).astype(jnp.int32),
        "first_scale": jnp.clip(jnp.exp(math.log(0.5) - 2.3025851 * jax.random.uniform(splits[5], (D // QROWS, KV // QCOLS), jnp.float32) ** level_of(splits[5], (D // QROWS, KV // QCOLS), ((0, 64), (1, 4)), -0.2, 0.2)), 0.05, 0.5),
        "second_scale": jnp.clip(jnp.exp(math.log(0.2) - 2.3025851 * jax.random.uniform(splits[6], (D // QROWS, KV // QCOLS), jnp.float32) ** level_of(splits[6], (D // QROWS, KV // QCOLS), ((0, 64), (1, 4)), -0.2, 0.2)), 0.02, 0.2),
    }


beta_one = 0.9
beta_two = 0.95
learn_rate = 0.002
weight_decay = 0.1
epsilon = 1e-08
clip_rms = 0.25

def blocks(array):
    return array.reshape(array.shape[0] // QROWS, QROWS, array.shape[1] // QCOLS, QCOLS)

def adam_step(gradient, norm_sq, master, first_codes, second_codes, first_scale, second_scale):
    factor = jnp.minimum(1.0, clip_rms * math.sqrt(D * KV) / (jnp.sqrt(norm_sq) + 1e-06))
    clipped = blocks(gradient * factor)
    first_old = blocks(first_codes.astype(jnp.float32)) / 127.0 * first_scale[:, None, :, None]
    second_old = blocks(second_codes.astype(jnp.float32)) / 255.0 * second_scale[:, None, :, None]
    first_new = beta_one * first_old + (1.0 - beta_one) * clipped
    second_new = beta_two * second_old + (1.0 - beta_two) * clipped * clipped
    first_hat = first_new / (1.0 - beta_one ** STEP)
    second_hat = second_new / (1.0 - beta_two ** STEP)
    step_dir = (first_hat / (jnp.sqrt(second_hat) + epsilon)).reshape(master.shape)
    new_master = master - learn_rate * (step_dir + weight_decay * master)
    first_top = lax.optimization_barrier(jnp.max(jnp.abs(first_new), axis=(1, 3))) + 1e-06
    second_top = lax.optimization_barrier(jnp.max(second_new, axis=(1, 3))) + 1e-06
    first_unit = (first_new / first_top[:, None, :, None]).reshape(master.shape)
    second_unit = (second_new / second_top[:, None, :, None]).reshape(master.shape)
    return (new_master, first_unit, second_unit, first_top, second_top)

def reference(inputs, key_cotangent, master, first_codes, second_codes, first_scale, second_scale):
    gradient = lax.dot_general(inputs, key_cotangent, (((0,), (0,)), ((), ())), preferred_element_type=jnp.float32)
    norm_sq = jnp.sum(gradient * gradient)
    new_master, first_unit, second_unit, first_top, second_top = adam_step(gradient, norm_sq, master, first_codes, second_codes, first_scale, second_scale)
    weight = new_master.astype(jnp.bfloat16)
    return (weight, new_master, first_unit, second_unit, first_top, second_top)
```

```python
import math

import jax
import jax.numpy as jnp
from jax import lax
from jax.sharding import Mesh
from jax.sharding import PartitionSpec as P

D = 4608
KV = 2048
QROWS = 4
QCOLS = 512
STEP = 10
X, Z, C, Y = "dp_0", "dp_1", "dp_2", "mp"
SIZE = {X: 4, Z: 8, C: 2, Y: 4}
DP = (X, Z, C)

beta_one = 0.9
beta_two = 0.95
learn_rate = 0.002
weight_decay = 0.1
epsilon = 1e-08
clip_rms = 0.25

f32 = jnp.float32


def shift(value, axis, by):
    n = SIZE[axis]
    return lax.ppermute(value, axis, [(i, (i + by) % n) for i in range(n)])


def swap(value):
    return lax.ppermute(value, C, [(0, 1), (1, 0)])


def ring_reduce_scatter(get, axis):
    m = SIZE[axis] // 2
    sums = [get(0, 0), get(0, 1)]
    arrived = {}
    for by in (1, -1):
        first = 0 if by == 1 else 1
        arrived[by] = {first: shift(get(by * m, first), axis, by)}
    for k in range(m - 1, 0, -1):
        for turn in (1, 0):
            for by in (1, -1):
                h = turn if by == 1 else 1 - turn
                term = get(by * k, h)
                if h in arrived[by]:
                    term = term + arrived[by][h]
                arrived[by][h] = shift(term, axis, by)
    return [sums[h] + arrived[1][h] + arrived[-1][h] for h in (0, 1)]


def ring_gather(halves, axis):
    m = SIZE[axis] // 2
    found = {(0, h): halves[h] for h in (0, 1)}
    for k in range(1, m + 1):
        for turn in (0, 1):
            for by in (1, -1):
                h = turn if by == 1 else 1 - turn
                if k == m and turn == 1:
                    continue
                found[(-by * k, h)] = shift(found[(-by * (k - 1), h)], axis, by)
    return {(k % SIZE[axis], h): v for (k, h), v in found.items()}


def placed(pieces, axis, dim):
    n = SIZE[axis]
    at = lax.axis_index(axis)
    stacked = jnp.stack([pieces[k] for k in range(n)], axis=dim)
    return jnp.roll(stacked, at, axis=dim)


def total_over_all(value):
    spread = jnp.broadcast_to(value, (16, 8, 128))
    part = jnp.sum(lax.all_to_all(spread, (Z, C), 0, 0, tiled=True)[:, 0, 0])
    spread = jnp.broadcast_to(part, (16, 8, 128))
    return jnp.sum(lax.all_to_all(spread, (X, Y), 0, 0, tiled=True)[:, 0, 0])


def per_row(scale):
    return jnp.repeat(scale, QROWS, axis=0)


def moments(gradient, factor, first_old, second_old):
    clipped = gradient * factor
    first_new = beta_one * first_old + (1.0 - beta_one) * clipped
    second_new = beta_two * second_old + (1.0 - beta_two) * clipped * clipped
    return first_new, second_new


def stepped(master, first_new, second_new):
    first_hat = first_new / (1.0 - beta_one**STEP)
    second_hat = second_new / (1.0 - beta_two**STEP)
    step_dir = first_hat / (jnp.sqrt(second_hat) + epsilon)
    return master - learn_rate * (step_dir + weight_decay * master)


def shards(inputs, key_cotangent, master, first_codes, second_codes, first_scale, second_scale):
    x, z, c = (lax.axis_index(a) for a in DP)
    contract = (((0,), (0,)), ((), ()))

    def half_of(array, which):
        return lax.dynamic_slice_in_dim(array, which * 256, 256, axis=array.ndim - 1)

    def term(which):
        return lax.dot_general(inputs, half_of(key_cotangent, which), contract, preferred_element_type=f32)

    theirs = swap(term(1 - c))
    mine = term(c) + theirs

    first_old = first_codes.astype(f32) / 127.0 * per_row(first_scale)
    second_old = second_codes.astype(f32) / 255.0 * per_row(second_scale)
    state = jnp.stack([master, first_old, second_old])
    own = half_of(state, c)
    got = swap(half_of(state, 1 - c))
    both = jnp.concatenate([jnp.where(c == 0, own, got), jnp.where(c == 0, got, own)], axis=1)

    part_a = mine[:, :128].reshape(4, 8, 144, 128)
    part_b = mine[:, 128:].reshape(4, 8, 144, 128)

    def row_a(k, h):
        return lax.dynamic_slice(part_a, ((x + k) % 4, 4 * h, 0, 0), (1, 4, 144, 128))[0]

    def row_b(k, h):
        return lax.dynamic_slice(part_b, (2 * h, (z + k) % 8, 0, 0), (2, 1, 144, 128))[:, 0]

    over_x = jnp.concatenate(ring_reduce_scatter(row_a, X))
    over_z = jnp.concatenate(ring_reduce_scatter(row_b, Z))

    def next_a(k, h):
        return lax.dynamic_slice(over_x, ((z + k) % 8, 72 * h, 0), (1, 72, 128))[0]

    def next_b(k, h):
        return lax.dynamic_slice(over_z, ((x + k) % 4, 72 * h, 0), (1, 72, 128))[0]

    grad_a = jnp.concatenate(ring_reduce_scatter(next_a, Z))
    grad_b = jnp.concatenate(ring_reduce_scatter(next_b, X))
    norm_sq = total_over_all(jnp.sum(grad_a * grad_a) + jnp.sum(grad_b * grad_b))
    factor = jnp.minimum(1.0, clip_rms * math.sqrt(D * KV) / (jnp.sqrt(norm_sq) + 1e-06))

    gradient = jnp.concatenate([grad_a, grad_b], axis=1)
    weight = stepped(both[0], *moments(gradient, factor, both[1], both[2])).astype(jnp.bfloat16)

    kept = lax.dynamic_slice_in_dim(gradient, c * 72, 72, axis=0)
    came = swap(lax.dynamic_slice_in_dim(gradient, (1 - c) * 72, 72, axis=0))
    rows = jnp.concatenate([jnp.where(c == 0, kept, came), jnp.where(c == 0, came, kept)], axis=1)
    first_new, second_new = moments(rows, factor, first_old, second_old)
    new_master = stepped(master, first_new, second_new)
    first_top = jnp.max(jnp.abs(first_new).reshape(18, 4, 512), axis=(1, 2))[:, None] + 1e-06
    second_top = jnp.max(second_new.reshape(18, 4, 512), axis=(1, 2))[:, None] + 1e-06
    first_unit = first_new / per_row(first_top)
    second_unit = second_new / per_row(second_top)

    small_a = ring_gather([weight[:72, :128], weight[72:, :128]], Z)
    small_b = ring_gather([weight[:72, 128:], weight[72:, 128:]], X)
    full_a = placed([jnp.concatenate([small_a[(k, 0)], small_a[(k, 1)]]) for k in range(8)], Z, 0)
    full_b = placed([jnp.concatenate([small_b[(k, 0)], small_b[(k, 1)]]) for k in range(4)], X, 0)
    large_a = ring_gather([full_a[:4], full_a[4:]], X)
    large_b = ring_gather([full_b[:2], full_b[2:]], Z)
    all_a = placed([jnp.concatenate([large_a[(k, 0)], large_a[(k, 1)]]) for k in range(4)], X, 0)
    all_b = placed([jnp.concatenate([large_b[(k, 0)], large_b[(k, 1)]]) for k in range(8)], Z, 1)
    held = jnp.concatenate([all_a.reshape(D, 128), all_b.reshape(D, 128)], axis=1)
    other = swap(held)
    out = jnp.concatenate([jnp.where(c == 0, held, other), jnp.where(c == 0, other, held)], axis=1)
    return (out, new_master, first_unit, second_unit, first_top, second_top)


def solution(mesh):
    finer = Mesh(mesh.devices.reshape(4, 8, 2, mesh.shape["mp"]), (X, Z, C, Y))
    in_specs = (P(DP, None),) + (P(DP, Y),) * 6
    out_specs = (P(None, Y),) + (P(DP, Y),) * 5
    return jax.shard_map(shards, mesh=finer, in_specs=in_specs, out_specs=out_specs, check_vma=False)
```

```python
import math

import jax
import jax.numpy as jnp
import numpy as np
from jax import lax
from jax.experimental import pallas as pl
from jax.experimental.pallas import tpu as pltpu
from jax.sharding import Mesh
from jax.sharding import PartitionSpec as P

D = 4608
KV = 2048
QROWS = 4
QCOLS = 512
STEP = 10
X, Z, C, Y = "dp_0", "dp_1", "dp_2", "mp"
SIZE = {X: 4, Z: 8, C: 2, Y: 4}
DP = (X, Z, C)

beta_one = 0.9
beta_two = 0.95
learn_rate = 0.002
weight_decay = 0.1
epsilon = 1e-08
clip_rms = 0.25

f32 = jnp.float32


MATES = {
    X: ((1, 0, 3, 2), (3, 2, 1, 0)),
    Z: ((1, 0, 3, 2, 5, 4, 7, 6), (7, 2, 1, 4, 3, 6, 5, 0), (3, 6, 5, 0, 7, 2, 1, 4)),
}


def swap(value):
    return lax.ppermute(value, C, [(0, 1), (1, 0)])


def exchange(value, axis, step):
    n = SIZE[axis]
    mate = MATES[axis][step]
    pairs = [(i * 2 + c, ((mate[(i - c) % n] + c) % n) * 2 + c) for i in range(n) for c in range(2)]
    return lax.ppermute(value, (axis, C), pairs)


def kept_order(axis, node, step):
    if step == len(MATES[axis]):
        return [node]
    return kept_order(axis, node, step + 1) + kept_order(axis, MATES[axis][step][node], step + 1)


def order_of(axis, core):
    n = SIZE[axis]
    table = np.array([[[(d + c) % n for d in kept_order(axis, (i - c) % n, 0)] for c in range(2)] for i in range(n)], np.int32)
    return jnp.asarray(table)[lax.axis_index(axis), core]


def halving_sum(send, keep, axis, first=0):
    for step in range(first, len(MATES[axis])):
        if step > first:
            half = keep.shape[0] // 2
            send, keep = keep[half:], keep[:half]
        keep = keep + exchange(send, axis, step)
    return keep


def doubling_gather(value, axis):
    for step in range(len(MATES[axis]) - 1, -1, -1):
        value = jnp.concatenate([value, exchange(value, axis, step)])
    return value


def packed(mine, theirs, order_x, order_z, keep):
    def kernel(ox, oz, p, q, a, b):
        for i in range(4):
            for j in range(8):
                at = pl.ds(pl.multiple_of((ox[i] * 8 + oz[j]) * 144, 8), 144)
                if (i < 2) == keep:
                    a[i % 2, j] = p[at, :128] + q[at, :128]
                if (j < 4) == keep:
                    b[j % 4, i] = p[at, 128:] + q[at, 128:]

    smem, vmem = pl.BlockSpec(memory_space=pltpu.SMEM), pl.BlockSpec(memory_space=pltpu.VMEM)
    return pl.pallas_call(
        kernel,
        in_specs=[smem, smem, vmem, vmem],
        out_specs=[vmem, vmem],
        out_shape=[jax.ShapeDtypeStruct((2, 8, 144, 128), f32), jax.ShapeDtypeStruct((4, 4, 144, 128), f32)],
        compiler_params=pltpu.CompilerParams(vmem_limit_bytes=40 << 20),
        cost_estimate=pl.CostEstimate(flops=0, bytes_accessed=7 << 20, transcendentals=0),
    )(order_x, order_z, mine, theirs)


def assembled(a, b, other_a, other_b, orders, core):
    def kernel(ox, oz, px, pz, me, a, b, c, d, out, sem):
        copies = []
        mine = pl.multiple_of(me[0] * 256, 128)
        other = pl.multiple_of((1 - me[0]) * 256, 128)
        for source, x_order, z_order, col in ((a, ox, oz, mine), (c, px, pz, other)):
            for i in range(4):
                for j in range(8):
                    copies.append((source.at[i, j], (x_order[i], z_order[j], col)))
        for source, x_order, z_order, col in ((b, ox, oz, mine + 128), (d, px, pz, other + 128)):
            for i in range(4):
                for j in range(8):
                    copies.append((source.at[j, i], (x_order[i], z_order[j], col)))
        started = []
        for n, (source, (xi, zi, col)) in enumerate(copies):
            rows = pl.ds(pl.multiple_of((xi * 8 + zi) * 144, 16), 144)
            copy = pltpu.make_async_copy(source, out.at[rows, pl.ds(pl.multiple_of(col, 128), 128)], sem.at[n])
            copy.start()
            started.append(copy)
        for copy in started:
            copy.wait()

    smem, vmem = pl.BlockSpec(memory_space=pltpu.SMEM), pl.BlockSpec(memory_space=pltpu.VMEM)
    return pl.pallas_call(
        kernel,
        in_specs=[smem] * 5 + [vmem] * 4,
        out_specs=pl.BlockSpec(memory_space=pl.ANY),
        out_shape=jax.ShapeDtypeStruct((D, 512), jnp.bfloat16),
        scratch_shapes=[pltpu.SemaphoreType.DMA((128,))],
        compiler_params=pltpu.CompilerParams(vmem_limit_bytes=24 << 20),
        cost_estimate=pl.CostEstimate(flops=0, bytes_accessed=9 << 20, transcendentals=0),
    )(*orders, core.reshape(1), a, b, other_a, other_b)


def total_over_all(value):
    spread = jnp.broadcast_to(value, (16, 8, 128))
    part = jnp.sum(lax.all_to_all(spread, (Z, C), 0, 0, tiled=True)[:, 0, 0])
    spread = jnp.broadcast_to(part, (16, 8, 128))
    return jnp.sum(lax.all_to_all(spread, (X, Y), 0, 0, tiled=True)[:, 0, 0])


def per_row(scale):
    return jnp.repeat(scale, QROWS, axis=0)


def moments(gradient, factor, first_old, second_old):
    clipped = gradient * factor
    first_new = beta_one * first_old + (1.0 - beta_one) * clipped
    second_new = beta_two * second_old + (1.0 - beta_two) * clipped * clipped
    return first_new, second_new


def stepped(master, first_new, second_new):
    first_hat = first_new / (1.0 - beta_one**STEP)
    second_hat = second_new / (1.0 - beta_two**STEP)
    step_dir = first_hat / (jnp.sqrt(second_hat) + epsilon)
    return master - learn_rate * (step_dir + weight_decay * master)


def shards(inputs, key_cotangent, master, first_codes, second_codes, first_scale, second_scale):
    x, z, c = (lax.axis_index(a) for a in DP)
    contract = (((0,), (0,)), ((), ()))

    def half_of(array, which):
        return lax.dynamic_slice_in_dim(array, which * 256, 256, axis=array.ndim - 1)

    def term(which):
        return lax.dot_general(inputs, half_of(key_cotangent, which), contract, preferred_element_type=f32)

    theirs = swap(term(1 - c))
    mine = lax.optimization_barrier(term(c))
    order_x, order_z = order_of(X, c), order_of(Z, c)

    first_old = first_codes.astype(f32) / 127.0 * per_row(first_scale)
    second_old = second_codes.astype(f32) / 255.0 * per_row(second_scale)
    state = jnp.stack([master, first_old, second_old])
    own = half_of(state, c)
    got = swap(half_of(state, 1 - c))
    both = jnp.concatenate([jnp.where(c == 0, own, got), jnp.where(c == 0, got, own)], axis=1)

    send_a, send_b = packed(mine, theirs, order_x, order_z, False)
    keep_a, keep_b = packed(mine, theirs, order_x, order_z, True)
    over_x = halving_sum(send_a, keep_a, X)[0]
    over_z = halving_sum(send_b, keep_b, Z)[0]
    grad_a = halving_sum(over_x[4:], over_x[:4], Z)[0]
    grad_b = halving_sum(over_z[2:], over_z[:2], X)[0]
    norm_sq = total_over_all(jnp.sum(grad_a * grad_a) + jnp.sum(grad_b * grad_b))
    factor = jnp.minimum(1.0, clip_rms * math.sqrt(D * KV) / (jnp.sqrt(norm_sq) + 1e-06))

    gradient = jnp.concatenate([grad_a, grad_b], axis=1)
    weight = stepped(both[0], *moments(gradient, factor, both[1], both[2])).astype(jnp.bfloat16)

    kept = lax.dynamic_slice_in_dim(gradient, c * 72, 72, axis=0)
    came = swap(lax.dynamic_slice_in_dim(gradient, (1 - c) * 72, 72, axis=0))
    rows = jnp.concatenate([jnp.where(c == 0, kept, came), jnp.where(c == 0, came, kept)], axis=1)
    first_new, second_new = moments(rows, factor, first_old, second_old)
    new_master = stepped(master, first_new, second_new)
    first_top = jnp.max(jnp.abs(first_new).reshape(18, 4, 512), axis=(1, 2))[:, None] + 1e-06
    second_top = jnp.max(second_new.reshape(18, 4, 512), axis=(1, 2))[:, None] + 1e-06
    first_unit = first_new / per_row(first_top)
    second_unit = second_new / per_row(second_top)

    all_a = doubling_gather(doubling_gather(weight[None, :, :128], Z)[None], X)
    all_b = doubling_gather(doubling_gather(weight[None, :, 128:], X)[None], Z)
    orders = (order_x, order_z, order_of(X, 1 - c), order_of(Z, 1 - c))
    out = assembled(all_a, all_b, swap(all_a), swap(all_b), orders, c)
    return (out, new_master, first_unit, second_unit, first_top, second_top)


def solution(mesh):
    finer = Mesh(mesh.devices.reshape(4, 8, 2, mesh.shape["mp"]), (X, Z, C, Y))
    in_specs = (P(DP, None),) + (P(DP, Y),) * 6
    out_specs = (P(None, Y),) + (P(DP, Y),) * 5
    return jax.shard_map(shards, mesh=finer, in_specs=in_specs, out_specs=out_specs, check_vma=False)
```

```python
import math

import jax
import jax.numpy as jnp
import numpy as np
from jax import lax
from jax.experimental import pallas as pl
from jax.experimental.pallas import tpu as pltpu
from jax.sharding import Mesh
from jax.sharding import PartitionSpec as P

D = 4608
KV = 2048
QROWS = 4
QCOLS = 512
STEP = 10
X, Z, C, Y = "dp_0", "dp_1", "dp_2", "mp"
SIZE = {X: 4, Z: 8, C: 2, Y: 4}
DP = (X, Z, C)

beta_one = 0.9
beta_two = 0.95
learn_rate = 0.002
weight_decay = 0.1
epsilon = 1e-08
clip_rms = 0.25

f32 = jnp.float32


MATES = {
    X: ((1, 0, 3, 2), (3, 2, 1, 0)),
    Z: ((1, 0, 3, 2, 5, 4, 7, 6), (7, 2, 1, 4, 3, 6, 5, 0), (3, 6, 5, 0, 7, 2, 1, 4)),
}


def swap(value):
    return lax.ppermute(value, C, [(0, 1), (1, 0)])


def exchange(value, axis, step):
    n = SIZE[axis]
    mate = MATES[axis][step]
    pairs = [(i * 2 + c, ((mate[(i - c) % n] + c) % n) * 2 + c) for i in range(n) for c in range(2)]
    return lax.ppermute(value, (axis, C), pairs)


def kept_order(axis, node, step):
    if step == len(MATES[axis]):
        return [node]
    return kept_order(axis, node, step + 1) + kept_order(axis, MATES[axis][step][node], step + 1)


def order_of(axis, core):
    n = SIZE[axis]
    table = np.array([[[(d + c) % n for d in kept_order(axis, (i - c) % n, 0)] for c in range(2)] for i in range(n)], np.int32)
    return jnp.asarray(table)[lax.axis_index(axis), core]


def sent_half(send, axis, step, terms):
    return exchange((send * (1.0 / terms)).astype(jnp.float16), axis, step).astype(f32) * float(terms)


def halving_sum(send, keep, axis, terms):
    for step in range(len(MATES[axis])):
        if step:
            half = keep.shape[0] // 2
            send, keep = keep[half:], keep[:half]
        keep = keep + sent_half(send, axis, step, terms)
        terms *= 2
    return keep[0]


def doubling_gather(value, axis, last=0):
    for step in range(len(MATES[axis]) - 1, last - 1, -1):
        value = jnp.concatenate([value, exchange(value, axis, step)])
    return value


def products(inputs, key_cotangent, core, h):
    width = 1152

    def kernel(me, a, b, theirs, mine, buf, sem):
        copies = [pltpu.make_async_copy(a.at[:, pl.ds(h * 2304 + i * width, width)], buf.at[i], sem.at[i]) for i in (0, 1)]
        for copy in copies:
            copy.start()
        for i in (0, 1):
            copies[i].wait()
            term = lax.dot_general(buf[i], b[...], (((0,), (0,)), ((), ())), preferred_element_type=f32)
            at = pl.ds(i * width, width)
            for c, left, right in ((0, mine, theirs), (1, theirs, mine)):

                @pl.when(me[0] == c)
                def _(left=left, right=right):
                    left[at, :] = term[:, :256]
                    right[at, :] = term[:, 256:]

    smem, vmem = pl.BlockSpec(memory_space=pltpu.SMEM), pl.BlockSpec(memory_space=pltpu.VMEM)
    return pl.pallas_call(
        kernel,
        in_specs=[smem, pl.BlockSpec(memory_space=pl.ANY), vmem],
        out_specs=[vmem, vmem],
        out_shape=[jax.ShapeDtypeStruct((2304, 256), f32)] * 2,
        scratch_shapes=[pltpu.VMEM((2, 768, width), jnp.bfloat16), pltpu.SemaphoreType.DMA((2,))],
        compiler_params=pltpu.CompilerParams(vmem_limit_bytes=24 << 20),
        cost_estimate=pl.CostEstimate(flops=2 * 768 * 2304 * 512, bytes_accessed=9 << 20, transcendentals=0),
    )(core.reshape(1), inputs, key_cotangent)


def packed(mine, theirs, order_x, order_z, keep):
    def kernel(ox, oz, p0, p1, q0, q1, a, b):
        for i in range(4):
            for h, p, q in ((0, p0, q0), (1, p1, q1)):

                @pl.when(ox[i] // 2 == h)
                def _(i=i, h=h, p=p, q=q):
                    for j in range(8):
                        at = pl.ds(pl.multiple_of((ox[i] * 8 - h * 16 + oz[j]) * 144, 8), 144)
                        if (i < 2) == keep:
                            a[i % 2, j] = p[at, :128] + q[at, :128]
                        if (j < 4) == keep:
                            b[j % 4, i] = p[at, 128:] + q[at, 128:]

    smem, vmem = pl.BlockSpec(memory_space=pltpu.SMEM), pl.BlockSpec(memory_space=pltpu.VMEM)
    return pl.pallas_call(
        kernel,
        in_specs=[smem, smem] + [vmem] * 4,
        out_specs=[vmem, vmem],
        out_shape=[jax.ShapeDtypeStruct((2, 8, 144, 128), f32), jax.ShapeDtypeStruct((4, 4, 144, 128), f32)],
        compiler_params=pltpu.CompilerParams(vmem_limit_bytes=16 << 20),
        cost_estimate=pl.CostEstimate(flops=0, bytes_accessed=7 << 20, transcendentals=0),
    )(order_x, order_z, *mine, *theirs)


def written(out, pieces, orders, core, part):
    x_from, z_from = 2 * part, 4 * part

    def kernel(ox, oz, px, pz, me, a, b, c, d, *rest):
        out, sem = rest[-2:]
        mine = pl.multiple_of(me[0] * 256, 128)
        other = pl.multiple_of((1 - me[0]) * 256, 128)
        copies = []
        for source, x_order, z_order, col in ((a, ox, oz, mine), (c, px, pz, other)):
            copies += [(source.at[i, j], x_order[x_from + i], z_order[j], col) for i in range(2) for j in range(8)]
        for source, x_order, z_order, col in ((b, ox, oz, mine + 128), (d, px, pz, other + 128)):
            copies += [(source.at[j, i], x_order[i], z_order[z_from + j], col) for i in range(4) for j in range(4)]
        started = []
        for n, (source, xi, zi, col) in enumerate(copies):
            rows = pl.ds(pl.multiple_of((xi * 8 + zi) * 144, 16), 144)
            copy = pltpu.make_async_copy(source, out.at[rows, pl.ds(pl.multiple_of(col, 128), 128)], sem.at[n])
            copy.start()
            started.append(copy)
        for copy in started:
            copy.wait()

    smem, vmem = pl.BlockSpec(memory_space=pltpu.SMEM), pl.BlockSpec(memory_space=pltpu.VMEM)
    anywhere = pl.BlockSpec(memory_space=pl.ANY)
    held = [] if out is None else [out]
    return pl.pallas_call(
        kernel,
        in_specs=[smem] * 5 + [vmem] * 4 + [anywhere] * len(held),
        out_specs=anywhere,
        out_shape=jax.ShapeDtypeStruct((D, 512), jnp.bfloat16),
        scratch_shapes=[pltpu.SemaphoreType.DMA((64,))],
        input_output_aliases={9: 0} if held else {},
        compiler_params=pltpu.CompilerParams(vmem_limit_bytes=8 << 20),
        cost_estimate=pl.CostEstimate(flops=0, bytes_accessed=9 << 20, transcendentals=0),
    )(*orders, core.reshape(1), *pieces, *held)


def total_over_all(value):
    spread = jnp.broadcast_to(value, (16, 8, 128))
    part = jnp.sum(lax.all_to_all(spread, (Z, C), 0, 0, tiled=True)[:, 0, 0])
    spread = jnp.broadcast_to(part, (16, 8, 128))
    return jnp.sum(lax.all_to_all(spread, (X, Y), 0, 0, tiled=True)[:, 0, 0])


def per_row(scale):
    return jnp.repeat(scale, QROWS, axis=0)


def moments(gradient, factor, first_old, second_old):
    clipped = gradient * factor
    first_new = beta_one * first_old + (1.0 - beta_one) * clipped
    second_new = beta_two * second_old + (1.0 - beta_two) * clipped * clipped
    return first_new, second_new


def stepped(master, first_new, second_new):
    first_hat = first_new / (1.0 - beta_one**STEP)
    second_hat = second_new / (1.0 - beta_two**STEP)
    step_dir = first_hat / (jnp.sqrt(second_hat) + epsilon)
    return master - learn_rate * (step_dir + weight_decay * master)


def weights_of(grad_a, grad_b, both, factor):
    def kernel(f, a, b, state, wa, wb):
        for grad, out, col in ((a, wa, 0), (b, wb, 128)):
            at = pl.ds(col, 128)
            news = moments(grad[...], f[0], state[1, :, at], state[2, :, at])
            out[...] = stepped(state[0, :, at], *news).astype(jnp.bfloat16)

    smem, vmem = pl.BlockSpec(memory_space=pltpu.SMEM), pl.BlockSpec(memory_space=pltpu.VMEM)
    return pl.pallas_call(
        kernel,
        in_specs=[smem] + [vmem] * 3,
        out_specs=[vmem, vmem],
        out_shape=[jax.ShapeDtypeStruct((144, 128), jnp.bfloat16)] * 2,
        compiler_params=pltpu.CompilerParams(vmem_limit_bytes=4 << 20),
        cost_estimate=pl.CostEstimate(flops=144 * 256 * 30, bytes_accessed=1 << 20, transcendentals=144 * 256),
    )(factor.reshape(1), grad_a, grad_b, both)


def own_results(left, right, state, factor):
    def largest(rows):
        top = jnp.broadcast_to(jnp.max(rows, axis=1, keepdims=True), (72, 128))
        at = lax.broadcasted_iota(jnp.int32, (72, 128), 0)
        top = jnp.maximum(top, jnp.where(at % 2 == 0, pltpu.roll(top, 71, 0), pltpu.roll(top, 1, 0)))
        return jnp.maximum(top, jnp.where(at % 4 < 2, pltpu.roll(top, 70, 0), pltpu.roll(top, 2, 0))) + 1e-06

    def kernel(f, l, r, state, master, first_unit, second_unit, first_top, second_top):
        gradient = jnp.concatenate([l[...], r[...]], axis=1)
        first_new, second_new = moments(gradient, f[0], state[1], state[2])
        master[...] = stepped(state[0], first_new, second_new)
        for new, unit, top in ((first_new, first_unit, first_top), (second_new, second_unit, second_top)):
            rows = largest(jnp.abs(new))
            top[...] = rows
            unit[...] = new / rows[:, :1]

    smem, vmem = pl.BlockSpec(memory_space=pltpu.SMEM), pl.BlockSpec(memory_space=pltpu.VMEM)
    return pl.pallas_call(
        kernel,
        in_specs=[smem] + [vmem] * 3,
        out_specs=[vmem] * 5,
        out_shape=[jax.ShapeDtypeStruct((72, 512), f32)] * 3 + [jax.ShapeDtypeStruct((72, 128), f32)] * 2,
        compiler_params=pltpu.CompilerParams(vmem_limit_bytes=8 << 20),
        cost_estimate=pl.CostEstimate(flops=72 * 512 * 40, bytes_accessed=1 << 20, transcendentals=72 * 512),
    )(factor.reshape(1), left, right, state)


def shards(inputs, key_cotangent, master, first_codes, second_codes, first_scale, second_scale):
    x, z, c = (lax.axis_index(a) for a in DP)
    order_x, order_z = order_of(X, c), order_of(Z, c)
    orders = (order_x, order_z, order_of(X, 1 - c), order_of(Z, 1 - c))

    terms = [products(inputs, key_cotangent, c, h) for h in (0, 1)]
    theirs = [swap(t) for t, _ in terms]
    mine = [m for _, m in terms]
    send_a, send_b = packed(mine, theirs, order_x, order_z, False)
    keep_a, keep_b = packed(mine, theirs, order_x, order_z, True)

    states = (master, first_codes, second_codes, first_scale, second_scale)
    keep_a, states = lax.optimization_barrier((keep_a, states))
    master, first_codes, second_codes, first_scale, second_scale = states
    first_old = first_codes.astype(f32) / 127.0 * per_row(first_scale)
    second_old = second_codes.astype(f32) / 255.0 * per_row(second_scale)
    state = jnp.stack([master, first_old, second_old])
    own = lax.dynamic_slice_in_dim(state, c * 256, 256, axis=2)
    got = swap(lax.dynamic_slice_in_dim(state, (1 - c) * 256, 256, axis=2))
    both = jnp.concatenate([jnp.where(c == 0, own, got), jnp.where(c == 0, got, own)], axis=1)

    over_x = halving_sum(send_a, keep_a, X, 2)
    over_z = halving_sum(send_b, keep_b, Z, 2)
    over_z, both = lax.optimization_barrier((over_z, both))
    grad_a = halving_sum(over_x[4:], over_x[:4], Z, 8)
    grad_b = halving_sum(over_z[2:], over_z[:2], X, 16)
    norm_sq = total_over_all(jnp.sum(grad_a * grad_a) + jnp.sum(grad_b * grad_b))
    factor = jnp.minimum(1.0, clip_rms * math.sqrt(D * KV) / (jnp.sqrt(norm_sq) + 1e-06))

    weight_a, weight_b = weights_of(grad_a, grad_b, both, factor)
    small_a, small_b = doubling_gather(weight_a[None], Z), doubling_gather(weight_b[None], X)

    gradient = jnp.concatenate([grad_a, grad_b], axis=1)
    kept = lax.dynamic_slice_in_dim(gradient, c * 72, 72, axis=0)
    came = swap(lax.dynamic_slice_in_dim(gradient, (1 - c) * 72, 72, axis=0))
    small_b, factor = lax.optimization_barrier((small_b, factor))
    left, right = jnp.where(c == 0, kept, came), jnp.where(c == 0, came, kept)
    new_master, first_unit, second_unit, first_top, second_top = own_results(left, right, state, factor)
    results = (new_master, first_unit, second_unit, first_top[::4, :1], second_top[::4, :1])

    near_a = doubling_gather(small_a[None], X, 1)
    near_b = doubling_gather(small_b[None], Z, 1)
    far_a, far_b = exchange(near_a, X, 0), exchange(near_b, Z, 0)
    near = (near_a, near_b, swap(near_a), swap(near_b))
    near, results = lax.optimization_barrier((near, results))
    out = written(None, near, orders, c, 0)
    out = written(out, (far_a, far_b, swap(far_a), swap(far_b)), orders, c, 1)
    return (out, *results)


def solution(mesh):
    finer = Mesh(mesh.devices.reshape(4, 8, 2, mesh.shape["mp"]), (X, Z, C, Y))
    in_specs = (P(DP, None),) + (P(DP, Y),) * 6
    out_specs = (P(None, Y),) + (P(DP, Y),) * 5
    return jax.shard_map(shards, mesh=finer, in_specs=in_specs, out_specs=out_specs, check_vma=False)
```

```python
import math

import jax
import jax.numpy as jnp
import numpy as np
from jax import lax
from jax.experimental import pallas as pl
from jax.experimental.pallas import tpu as pltpu
from jax.sharding import Mesh
from jax.sharding import PartitionSpec as P

D = 4608
KV = 2048
QROWS = 4
QCOLS = 512
STEP = 10
X, Z, C, Y = "dp_0", "dp_1", "dp_2", "mp"
SIZE = {X: 4, Z: 8, C: 2, Y: 4}
DP = (X, Z, C)

beta_one = 0.9
beta_two = 0.95
learn_rate = 0.002
weight_decay = 0.1
epsilon = 1e-08
clip_rms = 0.25

f32 = jnp.float32


MATES = {
    X: ((1, 0, 3, 2), (3, 2, 1, 0)),
    Z: ((1, 0, 3, 2, 5, 4, 7, 6), (7, 2, 1, 4, 3, 6, 5, 0), (3, 6, 5, 0, 7, 2, 1, 4)),
}


def swap(value):
    return lax.ppermute(value, C, [(0, 1), (1, 0)])


def exchange(value, axis, step):
    n = SIZE[axis]
    mate = MATES[axis][step]
    pairs = [(i * 2 + c, ((mate[(i - c) % n] + c) % n) * 2 + c) for i in range(n) for c in range(2)]
    return lax.ppermute(value, (axis, C), pairs)


def kept_order(axis, node, step):
    if step == len(MATES[axis]):
        return [node]
    return kept_order(axis, node, step + 1) + kept_order(axis, MATES[axis][step][node], step + 1)


def order_of(axis, core):
    n = SIZE[axis]
    table = np.array([[[(d + c) % n for d in kept_order(axis, (i - c) % n, 0)] for c in range(2)] for i in range(n)], np.int32)
    return jnp.asarray(table)[lax.axis_index(axis), core]


def narrowed(send, terms):
    return (send * (1.0 / terms)).astype(jnp.float16)


def halving_sum(send, keep, axis, terms):
    for step in range(len(MATES[axis])):
        if step:
            half = keep.shape[0] // 2
            send, keep = narrowed(keep[half:], terms), keep[:half]
        keep = keep + exchange(send, axis, step).astype(f32) * float(terms)
        terms *= 2
    return keep[0]


def doubling_gather(value, axis, last=0):
    for step in range(len(MATES[axis]) - 1, last - 1, -1):
        value = jnp.concatenate([value, exchange(value, axis, step)])
    return value


def products(inputs, key_cotangent, core, h):
    width = 1152

    def kernel(me, a, b, theirs, mine, buf, cot, sem):
        copies = [pltpu.make_async_copy(a.at[:, pl.ds(h * 2304 + i * width, width)], buf.at[i], sem.at[i]) for i in (0, 1)]
        for i, which in ((0, 1 - me[0]), (1, me[0])):
            at = pl.ds(pl.multiple_of(which * 256, 256), 256)
            copies.append(pltpu.make_async_copy(b.at[:, at], cot.at[:, pl.ds(i * 256, 256)], sem.at[2 + i]))
        for copy in copies:
            copy.start()
        copies[2].wait()
        copies[3].wait()
        for i in (0, 1):
            copies[i].wait()
            term = lax.dot_general(buf[i], cot[...], (((0,), (0,)), ((), ())), preferred_element_type=f32)
            theirs[pl.ds(i * width, width), :] = term[:, :256]
            mine[pl.ds(i * width, width), :] = term[:, 256:]

    smem, vmem = pl.BlockSpec(memory_space=pltpu.SMEM), pl.BlockSpec(memory_space=pltpu.VMEM)
    anywhere = pl.BlockSpec(memory_space=pl.ANY)
    return pl.pallas_call(
        kernel,
        in_specs=[smem, anywhere, anywhere],
        out_specs=[vmem, vmem],
        out_shape=[jax.ShapeDtypeStruct((2304, 256), f32)] * 2,
        scratch_shapes=[
            pltpu.VMEM((2, 768, width), jnp.bfloat16),
            pltpu.VMEM((768, 512), jnp.bfloat16),
            pltpu.SemaphoreType.DMA((4,)),
        ],
        compiler_params=pltpu.CompilerParams(vmem_limit_bytes=46 << 20),
        cost_estimate=pl.CostEstimate(flops=2 * 768 * 2304 * 512, bytes_accessed=9 << 20, transcendentals=0),
    )(core.reshape(1), inputs, key_cotangent)


def packed(mine, theirs, order_x, order_z, want_a, want_b):
    def kernel(ox, oz, p0, p1, q0, q1, *outs):
        for i in range(4):
            for h, p, q in ((0, p0, q0), (1, p1, q1)):

                @pl.when(ox[i] // 2 == h)
                def _(i=i, h=h, p=p, q=q):
                    for j in range(8):
                        at = pl.ds(pl.multiple_of((ox[i] * 8 - h * 16 + oz[j]) * 144, 8), 144)
                        if i // 2 == want_a:
                            outs[0][i % 2, j] = p[at, :128] + q[at, :128]
                        if j // 4 == want_b:
                            outs[-1][j % 4, i] = p[at, 128:] + q[at, 128:]

    smem, vmem = pl.BlockSpec(memory_space=pltpu.SMEM), pl.BlockSpec(memory_space=pltpu.VMEM)
    shapes = [(2, 8, 144, 128)] * (want_a is not None) + [(4, 4, 144, 128)] * (want_b is not None)
    return pl.pallas_call(
        kernel,
        in_specs=[smem, smem] + [vmem] * 4,
        out_specs=[vmem] * len(shapes),
        out_shape=[jax.ShapeDtypeStruct(shape, f32) for shape in shapes],
        compiler_params=pltpu.CompilerParams(vmem_limit_bytes=8 << 20),
        cost_estimate=pl.CostEstimate(flops=1024, bytes_accessed=4096, transcendentals=0),
    )(order_x, order_z, *mine, *theirs)


def written(pieces, orders, core):
    def kernel(ox, oz, px, pz, me, *rest):
        refs, out, sem = rest[:-2], rest[-2], rest[-1]
        mine = pl.multiple_of(me[0] * 256, 128)
        other = pl.multiple_of((1 - me[0]) * 256, 128)
        started = []
        for part in (0, 1):
            a, b, c, d = refs[4 * part : 4 * part + 4]
            for source, order, col in ((a, ox, mine), (c, px, other)):
                for i in (0, 1):
                    target = out.at[order[2 * part + i], :, :, pl.ds(pl.multiple_of(col, 128), 128)]
                    started.append(pltpu.make_async_copy(source.at[i], target, sem.at[len(started)]))
                    started[-1].start()
            for source, order, col in ((b, oz, mine), (d, pz, other)):
                for j in range(4):
                    target = out.at[:, order[4 * part + j], :, pl.ds(pl.multiple_of(col + 128, 128), 128)]
                    started.append(pltpu.make_async_copy(source.at[j], target, sem.at[len(started)]))
                    started[-1].start()
        for copy in started:
            copy.wait()

    smem, vmem = pl.BlockSpec(memory_space=pltpu.SMEM), pl.BlockSpec(memory_space=pltpu.VMEM)
    return pl.pallas_call(
        kernel,
        in_specs=[smem] * 5 + [vmem] * 8,
        out_specs=pl.BlockSpec(memory_space=pltpu.HBM),
        out_shape=jax.ShapeDtypeStruct((4, 8, 144, 512), jnp.bfloat16),
        scratch_shapes=[pltpu.SemaphoreType.DMA((24,))],
        compiler_params=pltpu.CompilerParams(vmem_limit_bytes=8 << 20),
        cost_estimate=pl.CostEstimate(flops=1024, bytes_accessed=4096, transcendentals=0),
    )(*orders, core.reshape(1), *pieces).reshape(D, 512)


def summed_over(value, axes):
    spread = jnp.broadcast_to(value, (16, 8, 128))
    return jnp.sum(lax.all_to_all(spread, axes, 0, 0, tiled=True)[:, 0, 0])


def per_row(scale):
    return jnp.repeat(scale, QROWS, axis=0)


def moments(gradient, factor, first_old, second_old):
    clipped = gradient * factor
    first_new = beta_one * first_old + (1.0 - beta_one) * clipped
    second_new = beta_two * second_old + (1.0 - beta_two) * clipped * clipped
    return first_new, second_new


def stepped(master, first_new, second_new):
    first_hat = first_new / (1.0 - beta_one**STEP)
    second_hat = second_new / (1.0 - beta_two**STEP)
    step_dir = first_hat / (jnp.sqrt(second_hat) + epsilon)
    return master - learn_rate * (step_dir + weight_decay * master)


def weights_of(planes_a, planes_b, order_x, factor):
    def kernel(ox, f, a0, a1, b0, b1, wa, wb):
        for source, out, place in ((a0, wa, (0, 1)), (a1, wa, (2, 3)), (b0, wb, (ox[0], ox[1])), (b1, wb, (ox[2], ox[3]))):
            for j in (0, 1):
                news = moments(source[j, 0], f[0], source[j, 2], source[j, 3])
                out[place[j]] = stepped(source[j, 1], *news).astype(jnp.bfloat16)

    smem, vmem = pl.BlockSpec(memory_space=pltpu.SMEM), pl.BlockSpec(memory_space=pltpu.VMEM)
    return pl.pallas_call(
        kernel,
        in_specs=[smem] * 2 + [vmem] * 4,
        out_specs=[vmem, vmem],
        out_shape=[jax.ShapeDtypeStruct((4, 144, 128), jnp.bfloat16)] * 2,
        compiler_params=pltpu.CompilerParams(vmem_limit_bytes=8 << 20),
        cost_estimate=pl.CostEstimate(flops=1024, bytes_accessed=4096, transcendentals=0),
    )(order_x, factor.reshape(1), *planes_a, *planes_b)


def by_place(first, second, order):
    def kernel(o, a, b, out):
        for j in range(8):
            out[o[j]] = (a if j < 4 else b)[j % 4]

    smem, vmem = pl.BlockSpec(memory_space=pltpu.SMEM), pl.BlockSpec(memory_space=pltpu.VMEM)
    return pl.pallas_call(
        kernel,
        in_specs=[smem, vmem, vmem],
        out_specs=vmem,
        out_shape=jax.ShapeDtypeStruct((8, 144, 128), jnp.bfloat16),
        compiler_params=pltpu.CompilerParams(vmem_limit_bytes=4 << 20),
        cost_estimate=pl.CostEstimate(flops=1024, bytes_accessed=4096, transcendentals=0),
    )(order, first, second)


def own_results(left, right, state, factor):
    def largest(rows):
        top = jnp.broadcast_to(jnp.max(rows, axis=1, keepdims=True), (72, 128))
        at = lax.broadcasted_iota(jnp.int32, (72, 128), 0)
        top = jnp.maximum(top, jnp.where(at % 2 == 0, pltpu.roll(top, 71, 0), pltpu.roll(top, 1, 0)))
        return jnp.maximum(top, jnp.where(at % 4 < 2, pltpu.roll(top, 70, 0), pltpu.roll(top, 2, 0))) + 1e-06

    def kernel(f, l, r, state, master, first_unit, second_unit, first_top, second_top):
        gradient = jnp.concatenate([l[...], r[...]], axis=1)
        first_new, second_new = moments(gradient, f[0], state[1], state[2])
        master[...] = stepped(state[0], first_new, second_new)
        for new, unit, top in ((first_new, first_unit, first_top), (second_new, second_unit, second_top)):
            rows = largest(jnp.abs(new))
            row_of = lax.broadcasted_iota(jnp.int32, (72, 128), 0)
            lane = lax.broadcasted_iota(jnp.int32, (72, 128), 1)
            picked = jnp.sum(jnp.where(row_of == 4 * lane, rows, 0.0), axis=0, keepdims=True)
            top[...] = picked[:, :18]
            unit[...] = new / rows[:, :1]

    smem, vmem = pl.BlockSpec(memory_space=pltpu.SMEM), pl.BlockSpec(memory_space=pltpu.VMEM)
    return pl.pallas_call(
        kernel,
        in_specs=[smem] + [vmem] * 3,
        out_specs=[vmem] * 5,
        out_shape=[jax.ShapeDtypeStruct((72, 512), f32)] * 3 + [jax.ShapeDtypeStruct((1, 18), f32)] * 2,
        compiler_params=pltpu.CompilerParams(vmem_limit_bytes=8 << 20),
        cost_estimate=pl.CostEstimate(flops=1024, bytes_accessed=4096, transcendentals=0),
    )(factor.reshape(1), left, right, state)


def shards(inputs, key_cotangent, master, first_codes, second_codes, first_scale, second_scale):
    x, z, c = (lax.axis_index(a) for a in DP)
    order_x, order_z = order_of(X, c), order_of(Z, c)
    orders = (order_x, order_z, order_of(X, 1 - c), order_of(Z, 1 - c))

    terms = [products(inputs, key_cotangent, c, h) for h in (0, 1)]
    theirs = [swap(t) for t, _ in terms]
    mine = [m for _, m in terms]
    send_b = narrowed(*packed(mine, theirs, order_x, order_z, None, 1), 2)
    send_b, mine = lax.optimization_barrier((send_b, mine))
    send_a = narrowed(*packed(mine, theirs, order_x, order_z, 1, None), 2)
    send_a, mine = lax.optimization_barrier((send_a, mine))
    keep_a, keep_b = packed(mine, theirs, order_x, order_z, 0, 0)

    states = (master, first_codes, second_codes, first_scale, second_scale)
    keep_a, states = lax.optimization_barrier((keep_a, states))
    master, first_codes, second_codes, first_scale, second_scale = states
    first_old = first_codes.astype(f32) / 127.0 * per_row(first_scale)
    second_old = second_codes.astype(f32) / 255.0 * per_row(second_scale)
    state = jnp.stack([master, first_old, second_old])
    own = lax.dynamic_slice_in_dim(state, c * 256, 256, axis=2)
    got = swap(lax.dynamic_slice_in_dim(state, (1 - c) * 256, 256, axis=2))
    both = jnp.concatenate([jnp.where(c == 0, own, got), jnp.where(c == 0, got, own)], axis=1)

    over_x = halving_sum(send_a, keep_a, X, 2)
    over_z = halving_sum(send_b, keep_b, Z, 2)
    over_x, both = lax.optimization_barrier((over_x, both))
    grad_a = halving_sum(narrowed(over_x[4:], 8), over_x[:4], Z, 8)
    grad_b = halving_sum(narrowed(over_z[2:], 16), over_z[:2], X, 16)

    planes_a = jnp.concatenate([grad_a[None], both[:, :, :128]])[None]
    planes_b = jnp.concatenate([grad_b[None], both[:, :, 128:]])[None]
    squares = summed_over(jnp.sum(grad_a * grad_a) + jnp.sum(grad_b * grad_b), (Z, C))
    met_a, met_b = exchange(planes_a, Z, 2), exchange(planes_b, X, 1)
    met_a, met_b, squares = lax.optimization_barrier((met_a, met_b, squares))
    norm_sq = summed_over(squares, (X, Y))
    near_planes_a = jnp.concatenate([planes_a, met_a])
    near_planes_b = jnp.concatenate([planes_b, met_b])
    far_planes_a = exchange(near_planes_a, Z, 1)
    far_planes_b = exchange(near_planes_b, X, 0)
    gradient = jnp.concatenate([grad_a, grad_b], axis=1)
    kept = lax.dynamic_slice_in_dim(gradient, c * 72, 72, axis=0)
    came = swap(lax.dynamic_slice_in_dim(gradient, (1 - c) * 72, 72, axis=0))
    left, right = jnp.where(c == 0, kept, came), jnp.where(c == 0, came, kept)

    factor = jnp.minimum(1.0, clip_rms * math.sqrt(D * KV) / (jnp.sqrt(norm_sq) + 1e-06))
    weight_a, weight_b = weights_of((near_planes_a, far_planes_a), (near_planes_b, far_planes_b), order_x, factor)
    far_z = exchange(weight_b[None], Z, 2)
    far_z, left, right, factor = lax.optimization_barrier((far_z, left, right, factor))
    new_master, first_unit, second_unit, first_top, second_top = own_results(left, right, state, factor)
    results = (new_master, first_unit, second_unit, first_top.reshape(18, 1), second_top.reshape(18, 1))

    column_a = by_place(weight_a, exchange(weight_a, Z, 0), order_z)
    near_a = doubling_gather(column_a[None], X, 1)
    near_a, results = lax.optimization_barrier((near_a, results))
    near_b = jnp.concatenate([weight_b[None], far_z])
    near_b = jnp.concatenate([near_b, exchange(near_b, Z, 1)])
    far_a, far_b = exchange(near_a, X, 0), exchange(near_b, Z, 0)
    pieces = (near_a, near_b, swap(near_a), swap(near_b), far_a, far_b, swap(far_a), swap(far_b))
    return (written(pieces, orders, c), *results)


def solution(mesh):
    finer = Mesh(mesh.devices.reshape(4, 8, 2, mesh.shape["mp"]), (X, Z, C, Y))
    in_specs = (P(DP, None),) + (P(DP, Y),) * 6
    out_specs = (P(None, Y),) + (P(DP, Y),) * 5
    return jax.shard_map(shards, mesh=finer, in_specs=in_specs, out_specs=out_specs, check_vma=False)
```

```python
import math

import jax
import jax.numpy as jnp
import numpy as np
from jax import lax
from jax.experimental import pallas as pl
from jax.experimental.pallas import tpu as pltpu
from jax.sharding import Mesh
from jax.sharding import PartitionSpec as P

D = 4608
KV = 2048
QROWS = 4
QCOLS = 512
STEP = 10
X, Z, C, Y = "dp_0", "dp_1", "dp_2", "mp"
SIZE = {X: 4, Z: 8, C: 2, Y: 4}
DP = (X, Z, C)

beta_one = 0.9
beta_two = 0.95
learn_rate = 0.002
weight_decay = 0.1
epsilon = 1e-08
clip_rms = 0.25

f32 = jnp.float32


MATES = {
    X: ((1, 0, 3, 2), (3, 2, 1, 0)),
    Z: ((1, 0, 3, 2, 5, 4, 7, 6), (7, 2, 1, 4, 3, 6, 5, 0), (3, 6, 5, 0, 7, 2, 1, 4)),
}


def swap(value):
    return lax.ppermute(value, C, [(0, 1), (1, 0)])


def exchange(value, axis, step):
    n = SIZE[axis]
    mate = MATES[axis][step]
    pairs = [(i * 2 + c, ((mate[(i - c) % n] + c) % n) * 2 + c) for i in range(n) for c in range(2)]
    return lax.ppermute(value, (axis, C), pairs)


def kept_order(axis, node, step):
    if step == len(MATES[axis]):
        return [node]
    return kept_order(axis, node, step + 1) + kept_order(axis, MATES[axis][step][node], step + 1)


def order_of(axis, core):
    n = SIZE[axis]
    table = np.array([[[(d + c) % n for d in kept_order(axis, (i - c) % n, 0)] for c in range(2)] for i in range(n)], np.int32)
    return jnp.asarray(table)[lax.axis_index(axis), core]


def narrowed(send, terms):
    return (send * (1.0 / terms)).astype(jnp.float16)


def halving_sum(came, keep, axis, terms):
    for step in range(len(MATES[axis])):
        if step:
            half = keep.shape[0] // 2
            came, keep = exchange(narrowed(keep[half:], terms), axis, step), keep[:half]
        keep = keep + came.astype(f32) * float(terms)
        terms *= 2
    return keep[0]


def doubling_gather(value, axis, last=0):
    for step in range(len(MATES[axis]) - 1, last - 1, -1):
        value = jnp.concatenate([value, exchange(value, axis, step)])
    return value


def products(inputs, key_cotangent, core, h):
    pieces = ((0, 384), (384, 1152), (1536, 768))

    def kernel(me, a, b, theirs, mine, buf, cot, term, sem):
        copies = []
        for i, which in ((0, 1 - me[0]), (1, me[0])):
            at = pl.ds(pl.multiple_of(which * 256, 256), 256)
            copies.append(pltpu.make_async_copy(b.at[:, at], cot.at[:, pl.ds(i * 256, 256)], sem.at[i]))
        for i, (at, width) in enumerate(pieces):
            copies.append(pltpu.make_async_copy(a.at[:, pl.ds(h * 2304 + at, width)], buf.at[:, pl.ds(at, width)], sem.at[2 + i]))
        for copy in copies:
            copy.start()
        copies[0].wait()
        copies[1].wait()
        away = []
        for i, (at, width) in enumerate(pieces):
            copies[2 + i].wait()
            rows = pl.ds(at, width)
            term[rows, :] = lax.dot_general(buf[:, at : at + width], cot[...], (((0,), (0,)), ((), ())), preferred_element_type=f32)
            for j, out in enumerate((theirs, mine)):
                away.append(pltpu.make_async_copy(term.at[rows, pl.ds(j * 256, 256)], out.at[rows, :], sem.at[5 + 2 * i + j]))
                away[-1].start()
        for copy in away:
            copy.wait()

    smem, anywhere = pl.BlockSpec(memory_space=pltpu.SMEM), pl.BlockSpec(memory_space=pl.ANY)
    return pl.pallas_call(
        kernel,
        in_specs=[smem, anywhere, anywhere],
        out_specs=[anywhere, anywhere],
        out_shape=[jax.ShapeDtypeStruct((2304, 256), f32)] * 2,
        scratch_shapes=[
            pltpu.VMEM((768, 2304), jnp.bfloat16),
            pltpu.VMEM((768, 512), jnp.bfloat16),
            pltpu.VMEM((2304, 512), f32),
            pltpu.SemaphoreType.DMA((11,)),
        ],
        compiler_params=pltpu.CompilerParams(vmem_limit_bytes=56 << 20),
        cost_estimate=pl.CostEstimate(flops=2 * 768 * 2304 * 512, bytes_accessed=9 << 20, transcendentals=0),
    )(core.reshape(1), inputs, key_cotangent)


def packed(mine, theirs, order_x, order_z, h, partly):
    def kernel(ox, oz, p, q, *rest):
        outs, held, sem = rest[-6:-2], rest[-2], rest[-1]
        copies = []
        for t in (0, 1):
            rows = pl.ds(t * 1152, 1152)
            for j, source in enumerate((p, q)):
                copies.append(pltpu.make_async_copy(source.at[rows, :], held.at[j, rows, :], sem.at[2 * t + j]))
        for copy in copies:
            copy.start()
        if partly:
            for i in range(4):

                @pl.when(ox[i] // 2 != h)
                def _(i=i):
                    outs[0 if i > 1 else 2][i % 2] = rest[0 if i > 1 else 2][i % 2]
                    outs[1][:, i] = rest[1][:, i]
                    outs[3][:, i] = rest[3][:, i]

        for t in (0, 1):
            copies[2 * t].wait()
            copies[2 * t + 1].wait()
            for i in range(4):

                @pl.when(ox[i] == 2 * h + t)
                def _(i=i, t=t):
                    for j in range(8):
                        at = pl.ds(pl.multiple_of(t * 1152 + oz[j] * 144, 8), 144)
                        outs[0 if i > 1 else 2][i % 2, j] = held[0, at, :128] + held[1, at, :128]
                        outs[1 if j > 3 else 3][j % 4, i] = held[0, at, 128:] + held[1, at, 128:]

    smem, vmem = pl.BlockSpec(memory_space=pltpu.SMEM), pl.BlockSpec(memory_space=pltpu.VMEM)
    anywhere = pl.BlockSpec(memory_space=pl.ANY)
    return pl.pallas_call(
        kernel,
        in_specs=[smem, smem, anywhere, anywhere] + [vmem] * len(partly),
        out_specs=[vmem] * 4,
        out_shape=[jax.ShapeDtypeStruct((2, 8, 144, 128), f32), jax.ShapeDtypeStruct((4, 4, 144, 128), f32)] * 2,
        scratch_shapes=[pltpu.VMEM((2, 2304, 256), f32), pltpu.SemaphoreType.DMA((4,))],
        compiler_params=pltpu.CompilerParams(vmem_limit_bytes=50 << 20),
        cost_estimate=pl.CostEstimate(flops=1024, bytes_accessed=4096, transcendentals=0),
    )(order_x, order_z, mine, theirs, *partly)


def written(pieces, orders, core):
    def kernel(ox, oz, px, pz, me, *rest):
        refs, out, sem = rest[:-2], rest[-2], rest[-1]
        mine = pl.multiple_of(me[0] * 256, 128)
        other = pl.multiple_of((1 - me[0]) * 256, 128)
        started = []
        for part in (0, 1):
            a, b, c, d = refs[4 * part : 4 * part + 4]
            for source, order, col in ((a, ox, mine), (c, px, other)):
                for i in (0, 1):
                    target = out.at[order[2 * part + i], :, :, pl.ds(pl.multiple_of(col, 128), 128)]
                    started.append(pltpu.make_async_copy(source.at[i], target, sem.at[len(started)]))
                    started[-1].start()
            for source, order, col in ((b, oz, mine), (d, pz, other)):
                for j in range(4):
                    target = out.at[:, order[4 * part + j], :, pl.ds(pl.multiple_of(col + 128, 128), 128)]
                    started.append(pltpu.make_async_copy(source.at[j], target, sem.at[len(started)]))
                    started[-1].start()
        for copy in started:
            copy.wait()

    smem, vmem = pl.BlockSpec(memory_space=pltpu.SMEM), pl.BlockSpec(memory_space=pltpu.VMEM)
    return pl.pallas_call(
        kernel,
        in_specs=[smem] * 5 + [vmem] * 8,
        out_specs=pl.BlockSpec(memory_space=pltpu.HBM),
        out_shape=jax.ShapeDtypeStruct((4, 8, 144, 512), jnp.bfloat16),
        scratch_shapes=[pltpu.SemaphoreType.DMA((24,))],
        compiler_params=pltpu.CompilerParams(vmem_limit_bytes=8 << 20),
        cost_estimate=pl.CostEstimate(flops=1024, bytes_accessed=4096, transcendentals=0),
    )(*orders, core.reshape(1), *pieces).reshape(D, 512)


def spread_squares(grad_a, grad_b):
    def kernel(a, b, out):
        out[...] = jnp.full(out.shape, jnp.sum(a[...] * a[...] + b[...] * b[...]), f32)

    return small_call(kernel, 16)(grad_a, grad_b)


def spread_sum(parts):
    def kernel(parts, out):
        out[...] = jnp.broadcast_to(jnp.sum(parts[:, :1], axis=0, keepdims=True), out.shape)

    return small_call(kernel, 16)(parts)


def small_call(kernel, rows):
    return pl.pallas_call(
        kernel,
        out_shape=jax.ShapeDtypeStruct((rows, 8, 128), f32),
        compiler_params=pltpu.CompilerParams(vmem_limit_bytes=4 << 20),
        cost_estimate=pl.CostEstimate(flops=1024, bytes_accessed=4096, transcendentals=0),
    )


def met(spread, axes):
    return lax.all_to_all(spread, axes, 0, 0, tiled=True)


def factor_of(parts):
    norm_sq = jnp.sum(parts[:, 0, :], axis=0, keepdims=True)
    return jnp.minimum(1.0, clip_rms * math.sqrt(D * KV) / (jnp.sqrt(norm_sq) + 1e-06))


def per_row(scale):
    return jnp.repeat(scale, QROWS, axis=0)


def moments(gradient, factor, first_old, second_old):
    clipped = gradient * factor
    first_new = beta_one * first_old + (1.0 - beta_one) * clipped
    second_new = beta_two * second_old + (1.0 - beta_two) * clipped * clipped
    return first_new, second_new


def stepped(master, first_new, second_new):
    first_hat = first_new / (1.0 - beta_one**STEP)
    second_hat = second_new / (1.0 - beta_two**STEP)
    step_dir = first_hat / (jnp.sqrt(second_hat) + epsilon)
    return master - learn_rate * (step_dir + weight_decay * master)


def weights_of(planes_a, planes_b, order_x, squares):
    def kernel(ox, f, a0, a1, b0, b1, wa, wb):
        factor = factor_of(f[...])
        for source, out, place in ((a0, wa, (0, 1)), (a1, wa, (2, 3)), (b0, wb, (ox[0], ox[1])), (b1, wb, (ox[2], ox[3]))):
            for j in (0, 1):
                news = moments(source[j, 0], factor, source[j, 2], source[j, 3])
                out[place[j]] = stepped(source[j, 1], *news).astype(jnp.bfloat16)

    smem, vmem = pl.BlockSpec(memory_space=pltpu.SMEM), pl.BlockSpec(memory_space=pltpu.VMEM)
    return pl.pallas_call(
        kernel,
        in_specs=[smem] + [vmem] * 5,
        out_specs=[vmem, vmem],
        out_shape=[jax.ShapeDtypeStruct((4, 144, 128), jnp.bfloat16)] * 2,
        compiler_params=pltpu.CompilerParams(vmem_limit_bytes=8 << 20),
        cost_estimate=pl.CostEstimate(flops=1024, bytes_accessed=4096, transcendentals=0),
    )(order_x, squares, *planes_a, *planes_b)


def by_place(first, second, order):
    def kernel(o, a, b, out):
        for j in range(8):
            out[o[j]] = (a if j < 4 else b)[j % 4]

    smem, vmem = pl.BlockSpec(memory_space=pltpu.SMEM), pl.BlockSpec(memory_space=pltpu.VMEM)
    return pl.pallas_call(
        kernel,
        in_specs=[smem, vmem, vmem],
        out_specs=vmem,
        out_shape=jax.ShapeDtypeStruct((8, 144, 128), jnp.bfloat16),
        compiler_params=pltpu.CompilerParams(vmem_limit_bytes=4 << 20),
        cost_estimate=pl.CostEstimate(flops=1024, bytes_accessed=4096, transcendentals=0),
    )(order, first, second)


def own_results(left, right, state, squares):
    def largest(rows):
        top = jnp.broadcast_to(jnp.max(rows, axis=1, keepdims=True), (72, 128))
        at = lax.broadcasted_iota(jnp.int32, (72, 128), 0)
        top = jnp.maximum(top, jnp.where(at % 2 == 0, pltpu.roll(top, 71, 0), pltpu.roll(top, 1, 0)))
        return jnp.maximum(top, jnp.where(at % 4 < 2, pltpu.roll(top, 70, 0), pltpu.roll(top, 2, 0))) + 1e-06

    def kernel(f, l, r, state, master, first_unit, second_unit, first_top, second_top):
        gradient = jnp.concatenate([l[...], r[...]], axis=1)
        first_new, second_new = moments(gradient, factor_of(f[...])[:, :1], state[1], state[2])
        master[...] = stepped(state[0], first_new, second_new)
        for new, unit, top in ((first_new, first_unit, first_top), (second_new, second_unit, second_top)):
            rows = largest(jnp.abs(new))
            row_of = lax.broadcasted_iota(jnp.int32, (72, 128), 0)
            lane = lax.broadcasted_iota(jnp.int32, (72, 128), 1)
            picked = jnp.sum(jnp.where(row_of == 4 * lane, rows, 0.0), axis=0, keepdims=True)
            top[...] = picked[:, :18]
            unit[...] = new / rows[:, :1]

    vmem = pl.BlockSpec(memory_space=pltpu.VMEM)
    return pl.pallas_call(
        kernel,
        in_specs=[vmem] * 4,
        out_specs=[vmem] * 5,
        out_shape=[jax.ShapeDtypeStruct((72, 512), f32)] * 3 + [jax.ShapeDtypeStruct((1, 18), f32)] * 2,
        compiler_params=pltpu.CompilerParams(vmem_limit_bytes=8 << 20),
        cost_estimate=pl.CostEstimate(flops=1024, bytes_accessed=4096, transcendentals=0),
    )(squares, left, right, state)


def shards(inputs, key_cotangent, master, first_codes, second_codes, first_scale, second_scale):
    x, z, c = (lax.axis_index(a) for a in DP)
    order_x, order_z = order_of(X, c), order_of(Z, c)
    orders = (order_x, order_z, order_of(X, 1 - c), order_of(Z, 1 - c))

    terms = [products(inputs, key_cotangent, c, h) for h in (0, 1)]
    parts = ()
    for h, (away, mine) in enumerate(terms):
        parts = packed(mine, swap(away), order_x, order_z, h, parts)
    send_a, send_b, keep_a, keep_b = parts

    come_b = exchange(narrowed(send_b, 2), Z, 0)
    come_a = exchange(narrowed(send_a, 2), X, 0)
    states = (master, first_codes, second_codes, first_scale, second_scale)
    come_b, states = lax.optimization_barrier((come_b, states))
    master, first_codes, second_codes, first_scale, second_scale = states
    first_old = first_codes.astype(f32) / 127.0 * per_row(first_scale)
    second_old = second_codes.astype(f32) / 255.0 * per_row(second_scale)
    state = jnp.stack([master, first_old, second_old])
    own = lax.dynamic_slice_in_dim(state, c * 256, 256, axis=2)
    got = swap(lax.dynamic_slice_in_dim(state, (1 - c) * 256, 256, axis=2))
    both = jnp.concatenate([jnp.where(c == 0, own, got), jnp.where(c == 0, got, own)], axis=1)

    over_x = halving_sum(come_a, keep_a, X, 2)
    over_z = halving_sum(come_b, keep_b, Z, 2)
    over_x, both = lax.optimization_barrier((over_x, both))
    grad_a = halving_sum(exchange(narrowed(over_x[4:], 8), Z, 0), over_x[:4], Z, 8)
    grad_b = halving_sum(exchange(narrowed(over_z[2:], 16), X, 0), over_z[:2], X, 16)

    planes_a = jnp.concatenate([grad_a[None], both[:, :, :128]])[None]
    planes_b = jnp.concatenate([grad_b[None], both[:, :, 128:]])[None]
    squares = met(spread_squares(grad_a, grad_b), (Z, C))
    met_a, met_b = exchange(planes_a, Z, 2), exchange(planes_b, X, 1)
    met_a, met_b, squares = lax.optimization_barrier((met_a, met_b, squares))
    squares = met(spread_sum(squares), (X, Y))
    near_planes_a = jnp.concatenate([planes_a, met_a])
    near_planes_b = jnp.concatenate([planes_b, met_b])
    far_planes_a = exchange(near_planes_a, Z, 1)
    far_planes_b = exchange(near_planes_b, X, 0)
    gradient = jnp.concatenate([grad_a, grad_b], axis=1)
    kept = lax.dynamic_slice_in_dim(gradient, c * 72, 72, axis=0)
    came = swap(lax.dynamic_slice_in_dim(gradient, (1 - c) * 72, 72, axis=0))
    left, right = jnp.where(c == 0, kept, came), jnp.where(c == 0, came, kept)

    weight_a, weight_b = weights_of((near_planes_a, far_planes_a), (near_planes_b, far_planes_b), order_x, squares)
    far_z = exchange(weight_b[None], Z, 2)
    far_z, left, right, squares = lax.optimization_barrier((far_z, left, right, squares))
    new_master, first_unit, second_unit, first_top, second_top = own_results(left, right, state, squares)
    results = (new_master, first_unit, second_unit, first_top.reshape(18, 1), second_top.reshape(18, 1))

    column_a = by_place(weight_a, exchange(weight_a, Z, 0), order_z)
    near_a = doubling_gather(column_a[None], X, 1)
    near_a, results = lax.optimization_barrier((near_a, results))
    near_b = jnp.concatenate([weight_b[None], far_z])
    near_b = jnp.concatenate([near_b, exchange(near_b, Z, 1)])
    far_a, far_b = exchange(near_a, X, 0), exchange(near_b, Z, 0)
    pieces = (near_a, near_b, swap(near_a), swap(near_b), far_a, far_b, swap(far_a), swap(far_b))
    return (written(pieces, orders, c), *results)


def solution(mesh):
    finer = Mesh(mesh.devices.reshape(4, 8, 2, mesh.shape["mp"]), (X, Z, C, Y))
    in_specs = (P(DP, None),) + (P(DP, Y),) * 6
    out_specs = (P(None, Y),) + (P(DP, Y),) * 5
    return jax.shard_map(shards, mesh=finer, in_specs=in_specs, out_specs=out_specs, check_vma=False)
```

```python
import math

import jax
import jax.numpy as jnp
import numpy as np
from jax import lax
from jax.experimental import pallas as pl
from jax.experimental.pallas import tpu as pltpu
from jax.sharding import Mesh
from jax.sharding import PartitionSpec as P

D = 4608
KV = 2048
QROWS = 4
QCOLS = 512
STEP = 10
X, Z, C, Y = "dp_0", "dp_1", "dp_2", "mp"
SIZE = {X: 4, Z: 8, C: 2, Y: 4}
DP = (X, Z, C)

beta_one = 0.9
beta_two = 0.95
learn_rate = 0.002
weight_decay = 0.1
epsilon = 1e-08
clip_rms = 0.25

f32 = jnp.float32


MATES = {
    X: ((1, 0, 3, 2), (3, 2, 1, 0)),
    Z: ((1, 0, 3, 2, 5, 4, 7, 6), (7, 2, 1, 4, 3, 6, 5, 0), (3, 6, 5, 0, 7, 2, 1, 4)),
}


def swap(value):
    return lax.ppermute(value, C, [(0, 1), (1, 0)])


def exchange(value, axis, step):
    n = SIZE[axis]
    mate = MATES[axis][step]
    pairs = [(i * 2 + c, ((mate[(i - c) % n] + c) % n) * 2 + c) for i in range(n) for c in range(2)]
    return lax.ppermute(value, (axis, C), pairs)


def kept_order(axis, node, step):
    if step == len(MATES[axis]):
        return [node]
    return kept_order(axis, node, step + 1) + kept_order(axis, MATES[axis][step][node], step + 1)


def order_of(axis, core):
    n = SIZE[axis]
    table = np.array([[[(d + c) % n for d in kept_order(axis, (i - c) % n, 0)] for c in range(2)] for i in range(n)], np.int32)
    return jnp.asarray(table)[lax.axis_index(axis), core]


def narrowed(send, terms):
    return (send * (1.0 / terms)).astype(jnp.float16)


def halving_sum(came, keep, axis, terms):
    for step in range(len(MATES[axis])):
        if step:
            half = keep.shape[0] // 2
            came, keep = exchange(narrowed(keep[half:], terms), axis, step), keep[:half]
        keep = keep + came.astype(f32) * float(terms)
        terms *= 2
    return keep[0]


def doubling_gather(value, axis, last=0):
    for step in range(len(MATES[axis]) - 1, last - 1, -1):
        value = jnp.concatenate([value, exchange(value, axis, step)])
    return value


def products(inputs, key_cotangent, core, h):
    pieces = ((0, 384), (384, 1152), (1536, 768))

    def kernel(me, a, b, theirs, mine, buf, cot, term, sem):
        copies = []
        for i, which in ((0, 1 - me[0]), (1, me[0])):
            at = pl.ds(pl.multiple_of(which * 256, 256), 256)
            copies.append(pltpu.make_async_copy(b.at[:, at], cot.at[:, pl.ds(i * 256, 256)], sem.at[i]))
        for i, (at, width) in enumerate(pieces):
            copies.append(pltpu.make_async_copy(a.at[:, pl.ds(h * 2304 + at, width)], buf.at[:, pl.ds(at, width)], sem.at[2 + i]))
        for copy in copies:
            copy.start()
        copies[0].wait()
        copies[1].wait()
        away = []
        for i, (at, width) in enumerate(pieces):
            copies[2 + i].wait()
            rows = pl.ds(at, width)
            term[rows, :] = lax.dot_general(buf[:, at : at + width], cot[...], (((0,), (0,)), ((), ())), preferred_element_type=f32)
            for j, out in enumerate((theirs, mine)):
                away.append(pltpu.make_async_copy(term.at[rows, pl.ds(j * 256, 256)], out.at[rows, :], sem.at[5 + 2 * i + j]))
                away[-1].start()
        for copy in away:
            copy.wait()

    smem, anywhere = pl.BlockSpec(memory_space=pltpu.SMEM), pl.BlockSpec(memory_space=pl.ANY)
    return pl.pallas_call(
        kernel,
        in_specs=[smem, anywhere, anywhere],
        out_specs=[anywhere, anywhere],
        out_shape=[jax.ShapeDtypeStruct((2304, 256), f32)] * 2,
        scratch_shapes=[
            pltpu.VMEM((768, 2304), jnp.bfloat16),
            pltpu.VMEM((768, 512), jnp.bfloat16),
            pltpu.VMEM((2304, 512), f32),
            pltpu.SemaphoreType.DMA((11,)),
        ],
        compiler_params=pltpu.CompilerParams(vmem_limit_bytes=56 << 20),
        cost_estimate=pl.CostEstimate(flops=2 * 768 * 2304 * 512, bytes_accessed=9 << 20, transcendentals=0),
    )(core.reshape(1), inputs, key_cotangent)


def packed(terms, theirs, order_x, order_z):
    def kernel(ox, oz, p0, p1, q0, q1, *rest):
        outs, held, sem = rest[:4], rest[4], rest[5]
        copies = []
        for h, pair in enumerate(((p0, q0), (p1, q1))):
            for t in (0, 1):
                for j, source in enumerate(pair):
                    rows = pl.ds(t * 1152, 1152)
                    target = held.at[j, pl.ds(h * 2304 + t * 1152, 1152), :]
                    copies.append(pltpu.make_async_copy(source.at[rows, :], target, sem.at[len(copies)]))
        for copy in copies:
            copy.start()
        for x in range(4):
            copies[2 * x].wait()
            copies[2 * x + 1].wait()
            for i in range(4):

                @pl.when(ox[i] == x)
                def _(i=i, x=x):
                    for j in range(8):
                        at = pl.ds(pl.multiple_of(x * 1152 + oz[j] * 144, 8), 144)
                        outs[0 if i > 1 else 2][i % 2, j] = held[0, at, :128] + held[1, at, :128]
                        outs[1 if j > 3 else 3][j % 4, i] = held[0, at, 128:] + held[1, at, 128:]

    smem, vmem = pl.BlockSpec(memory_space=pltpu.SMEM), pl.BlockSpec(memory_space=pltpu.VMEM)
    anywhere = pl.BlockSpec(memory_space=pl.ANY)
    return pl.pallas_call(
        kernel,
        in_specs=[smem, smem] + [anywhere] * 4,
        out_specs=[vmem] * 4,
        out_shape=[jax.ShapeDtypeStruct((2, 8, 144, 128), f32), jax.ShapeDtypeStruct((4, 4, 144, 128), f32)] * 2,
        scratch_shapes=[pltpu.VMEM((2, 4608, 256), f32), pltpu.SemaphoreType.DMA((8,))],
        compiler_params=pltpu.CompilerParams(vmem_limit_bytes=36 << 20),
        cost_estimate=pl.CostEstimate(flops=1024, bytes_accessed=4096, transcendentals=0),
    )(order_x, order_z, *[mine for _, mine in terms], *theirs)


def written(pieces, orders, core):
    def kernel(ox, oz, px, pz, me, *rest):
        refs, out, sem = rest[:-2], rest[-2], rest[-1]
        mine = pl.multiple_of(me[0] * 256, 128)
        other = pl.multiple_of((1 - me[0]) * 256, 128)
        started = []
        for part in (0, 1):
            a, b, c, d = refs[4 * part : 4 * part + 4]
            for source, order, col in ((a, ox, mine), (c, px, other)):
                for i in (0, 1):
                    target = out.at[order[2 * part + i], :, :, pl.ds(pl.multiple_of(col, 128), 128)]
                    started.append(pltpu.make_async_copy(source.at[i], target, sem.at[len(started)]))
                    started[-1].start()
            for source, order, col in ((b, oz, mine), (d, pz, other)):
                for j in range(4):
                    target = out.at[:, order[4 * part + j], :, pl.ds(pl.multiple_of(col + 128, 128), 128)]
                    started.append(pltpu.make_async_copy(source.at[j], target, sem.at[len(started)]))
                    started[-1].start()
        for copy in started:
            copy.wait()

    smem, vmem = pl.BlockSpec(memory_space=pltpu.SMEM), pl.BlockSpec(memory_space=pltpu.VMEM)
    return pl.pallas_call(
        kernel,
        in_specs=[smem] * 5 + [vmem] * 8,
        out_specs=pl.BlockSpec(memory_space=pltpu.HBM),
        out_shape=jax.ShapeDtypeStruct((4, 8, 144, 512), jnp.bfloat16),
        scratch_shapes=[pltpu.SemaphoreType.DMA((24,))],
        compiler_params=pltpu.CompilerParams(vmem_limit_bytes=8 << 20),
        cost_estimate=pl.CostEstimate(flops=1024, bytes_accessed=4096, transcendentals=0),
    )(*orders, core.reshape(1), *pieces).reshape(D, 512)


def spread_squares(grad_a, grad_b):
    def kernel(a, b, out):
        out[...] = jnp.full(out.shape, jnp.sum(a[...] * a[...] + b[...] * b[...]), f32)

    return small_call(kernel, 16)(grad_a, grad_b)


def spread_sum(parts):
    def kernel(parts, out):
        out[...] = jnp.broadcast_to(jnp.sum(parts[:, :1], axis=0, keepdims=True), out.shape)

    return small_call(kernel, 16)(parts)


def small_call(kernel, rows):
    return pl.pallas_call(
        kernel,
        out_shape=jax.ShapeDtypeStruct((rows, 8, 128), f32),
        compiler_params=pltpu.CompilerParams(vmem_limit_bytes=4 << 20),
        cost_estimate=pl.CostEstimate(flops=1024, bytes_accessed=4096, transcendentals=0),
    )


def met(spread, axes):
    return lax.all_to_all(spread, axes, 0, 0, tiled=True)


def factor_of(parts):
    norm_sq = jnp.sum(parts[:, 0, :], axis=0, keepdims=True)
    return jnp.minimum(1.0, clip_rms * math.sqrt(D * KV) / (jnp.sqrt(norm_sq) + 1e-06))


def per_row(scale):
    return jnp.repeat(scale, QROWS, axis=0)


def moments(gradient, factor, first_old, second_old):
    clipped = gradient * factor
    first_new = beta_one * first_old + (1.0 - beta_one) * clipped
    second_new = beta_two * second_old + (1.0 - beta_two) * clipped * clipped
    return first_new, second_new


def stepped(master, first_new, second_new):
    first_hat = first_new / (1.0 - beta_one**STEP)
    second_hat = second_new / (1.0 - beta_two**STEP)
    step_dir = first_hat / (jnp.sqrt(second_hat) + epsilon)
    return master - learn_rate * (step_dir + weight_decay * master)


def weights_of(planes_a, planes_b, order_x, squares):
    def kernel(ox, f, a0, a1, b0, b1, wa, wb):
        factor = factor_of(f[...])
        for source, out, place in ((a0, wa, (0, 1)), (a1, wa, (2, 3)), (b0, wb, (ox[0], ox[1])), (b1, wb, (ox[2], ox[3]))):
            for j in (0, 1):
                news = moments(source[j, 0], factor, source[j, 2], source[j, 3])
                out[place[j]] = stepped(source[j, 1], *news).astype(jnp.bfloat16)

    smem, vmem = pl.BlockSpec(memory_space=pltpu.SMEM), pl.BlockSpec(memory_space=pltpu.VMEM)
    return pl.pallas_call(
        kernel,
        in_specs=[smem] + [vmem] * 5,
        out_specs=[vmem, vmem],
        out_shape=[jax.ShapeDtypeStruct((4, 144, 128), jnp.bfloat16)] * 2,
        compiler_params=pltpu.CompilerParams(vmem_limit_bytes=8 << 20),
        cost_estimate=pl.CostEstimate(flops=1024, bytes_accessed=4096, transcendentals=0),
    )(order_x, squares, *planes_a, *planes_b)


def by_place(first, second, order):
    def kernel(o, a, b, out):
        for j in range(8):
            out[o[j]] = (a if j < 4 else b)[j % 4]

    smem, vmem = pl.BlockSpec(memory_space=pltpu.SMEM), pl.BlockSpec(memory_space=pltpu.VMEM)
    return pl.pallas_call(
        kernel,
        in_specs=[smem, vmem, vmem],
        out_specs=vmem,
        out_shape=jax.ShapeDtypeStruct((8, 144, 128), jnp.bfloat16),
        compiler_params=pltpu.CompilerParams(vmem_limit_bytes=4 << 20),
        cost_estimate=pl.CostEstimate(flops=1024, bytes_accessed=4096, transcendentals=0),
    )(order, first, second)


def own_results(left, right, state, squares):
    def largest(rows):
        top = jnp.broadcast_to(jnp.max(rows, axis=1, keepdims=True), (72, 128))
        at = lax.broadcasted_iota(jnp.int32, (72, 128), 0)
        top = jnp.maximum(top, jnp.where(at % 2 == 0, pltpu.roll(top, 71, 0), pltpu.roll(top, 1, 0)))
        return jnp.maximum(top, jnp.where(at % 4 < 2, pltpu.roll(top, 70, 0), pltpu.roll(top, 2, 0))) + 1e-06

    def kernel(f, l, r, state, master, first_unit, second_unit, first_top, second_top):
        gradient = jnp.concatenate([l[...], r[...]], axis=1)
        first_new, second_new = moments(gradient, factor_of(f[...])[:, :1], state[1], state[2])
        master[...] = stepped(state[0], first_new, second_new)
        for new, unit, top in ((first_new, first_unit, first_top), (second_new, second_unit, second_top)):
            rows = largest(jnp.abs(new))
            row_of = lax.broadcasted_iota(jnp.int32, (72, 128), 0)
            lane = lax.broadcasted_iota(jnp.int32, (72, 128), 1)
            picked = jnp.sum(jnp.where(row_of == 4 * lane, rows, 0.0), axis=0, keepdims=True)
            top[...] = picked[:, :18]
            unit[...] = new / rows[:, :1]

    vmem = pl.BlockSpec(memory_space=pltpu.VMEM)
    return pl.pallas_call(
        kernel,
        in_specs=[vmem] * 4,
        out_specs=[vmem] * 5,
        out_shape=[jax.ShapeDtypeStruct((72, 512), f32)] * 3 + [jax.ShapeDtypeStruct((1, 18), f32)] * 2,
        compiler_params=pltpu.CompilerParams(vmem_limit_bytes=8 << 20),
        cost_estimate=pl.CostEstimate(flops=1024, bytes_accessed=4096, transcendentals=0),
    )(squares, left, right, state)


def shards(inputs, key_cotangent, master, first_codes, second_codes, first_scale, second_scale):
    x, z, c = (lax.axis_index(a) for a in DP)
    order_x, order_z = order_of(X, c), order_of(Z, c)
    orders = (order_x, order_z, order_of(X, 1 - c), order_of(Z, 1 - c))

    terms = [products(inputs, key_cotangent, c, h) for h in (0, 1)]
    send_a, send_b, keep_a, keep_b = packed(terms, [swap(away) for away, _ in terms], order_x, order_z)

    come_b = exchange(narrowed(send_b, 2), Z, 0)
    come_a = exchange(narrowed(send_a, 2), X, 0)
    states = (master, first_codes, second_codes, first_scale, second_scale)
    come_b, states = lax.optimization_barrier((come_b, states))
    master, first_codes, second_codes, first_scale, second_scale = states
    first_old = first_codes.astype(f32) / 127.0 * per_row(first_scale)
    second_old = second_codes.astype(f32) / 255.0 * per_row(second_scale)
    state = jnp.stack([master, first_old, second_old])
    own = lax.dynamic_slice_in_dim(state, c * 256, 256, axis=2)
    got = swap(lax.dynamic_slice_in_dim(state, (1 - c) * 256, 256, axis=2))
    both = jnp.concatenate([jnp.where(c == 0, own, got), jnp.where(c == 0, got, own)], axis=1)

    over_x = halving_sum(come_a, keep_a, X, 2)
    over_z = halving_sum(come_b, keep_b, Z, 2)
    over_x, both = lax.optimization_barrier((over_x, both))
    grad_a = halving_sum(exchange(narrowed(over_x[4:], 8), Z, 0), over_x[:4], Z, 8)
    grad_b = halving_sum(exchange(narrowed(over_z[2:], 16), X, 0), over_z[:2], X, 16)

    planes_a = jnp.concatenate([grad_a[None], both[:, :, :128]])[None]
    planes_b = jnp.concatenate([grad_b[None], both[:, :, 128:]])[None]
    squares = met(spread_squares(grad_a, grad_b), (Z, C))
    met_a, met_b = exchange(planes_a, Z, 2), exchange(planes_b, X, 1)
    met_a, met_b, squares = lax.optimization_barrier((met_a, met_b, squares))
    squares = met(spread_sum(squares), (X, Y))
    near_planes_a = jnp.concatenate([planes_a, met_a])
    near_planes_b = jnp.concatenate([planes_b, met_b])
    far_planes_a = exchange(near_planes_a, Z, 1)
    far_planes_b = exchange(near_planes_b, X, 0)
    gradient = jnp.concatenate([grad_a, grad_b], axis=1)
    kept = lax.dynamic_slice_in_dim(gradient, c * 72, 72, axis=0)
    came = swap(lax.dynamic_slice_in_dim(gradient, (1 - c) * 72, 72, axis=0))
    left, right = jnp.where(c == 0, kept, came), jnp.where(c == 0, came, kept)

    weight_a, weight_b = weights_of((near_planes_a, far_planes_a), (near_planes_b, far_planes_b), order_x, squares)
    far_z = exchange(weight_b[None], Z, 2)
    far_z, left, right, squares = lax.optimization_barrier((far_z, left, right, squares))
    new_master, first_unit, second_unit, first_top, second_top = own_results(left, right, state, squares)
    results = (new_master, first_unit, second_unit, first_top.reshape(18, 1), second_top.reshape(18, 1))

    column_a = by_place(weight_a, exchange(weight_a, Z, 0), order_z)
    near_a = doubling_gather(column_a[None], X, 1)
    near_a, results = lax.optimization_barrier((near_a, results))
    near_b = jnp.concatenate([weight_b[None], far_z])
    near_b = jnp.concatenate([near_b, exchange(near_b, Z, 1)])
    far_a, far_b = exchange(near_a, X, 0), exchange(near_b, Z, 0)
    pieces = (near_a, near_b, swap(near_a), swap(near_b), far_a, far_b, swap(far_a), swap(far_b))
    return (written(pieces, orders, c), *results)


def solution(mesh):
    finer = Mesh(mesh.devices.reshape(4, 8, 2, mesh.shape["mp"]), (X, Z, C, Y))
    in_specs = (P(DP, None),) + (P(DP, Y),) * 6
    out_specs = (P(None, Y),) + (P(DP, Y),) * 5
    return jax.shard_map(shards, mesh=finer, in_specs=in_specs, out_specs=out_specs, check_vma=False)
```
